256 devices in a mesh: comp: 2 (over z_lo), tgt: 16 (over y, x), src: 8 (over z_hi, core).
Axes of the slice: x: 4, y: 4, z: 8 (z_hi: 4, z_lo: 2; z = z_hi * 2 + z_lo), core: 2. Of those that a mesh axis runs over, the one named last changes fastest.
Arguments:
- field: bfloat16 [3, 32, 65536], P(None, None, ('tgt', 'src')), may hold values from -6 to 6
- dest_group: int32 [32768, 1], P(('comp', 'tgt', 'src')), may hold values from 0 to 15; in each aligned block of 128 rows (0 to 127, 128 to 255, ...) at most 16 rows name the same one
- src_local: int32 [32768], P(('comp', 'tgt', 'src')), may hold values from 0 to 1
- ranks: int32 [32768], P(('comp', 'tgt', 'src')), may hold values from 8 to 64
- mixing: float32 [32768, 3, 3], P(('comp', 'tgt', 'src')), may hold values from -5 to 5
- v_factor: bfloat16 [32768, 64, 256], P(('comp', 'tgt', 'src')), may hold values from -0.375 to 0.375
- u_factor: bfloat16 [65536, 64, 256], P(('comp', 'tgt', 'src')), may hold values from -0.0625 to 0.0625
- slot_cluster: int32 [65536], P(('comp', 'tgt', 'src')), may hold values from 0 to 15
- near_src: int32 [1024], P(('comp', 'tgt', 'src')), may hold values from 0 to 1
- near_tgt: int32 [1024], P(('comp', 'tgt', 'src')), may hold values from 0 to 15
- near_mixing: float32 [1024, 3, 3], P(('comp', 'tgt', 'src')), may hold values from -5 to 5
- near_matrix: bfloat16 [1024, 256, 256], P(('comp', 'tgt', 'src')), may hold values from -0.1875 to 0.1875
Outputs:
- result: float32 [3, 32, 65536], P(None, None, ('comp', 'tgt', 'src'))
The draws below stay inside these ranges and needn't reach their ends.
Inputs may be any that keep to these rules, and one draw needn't show every extreme that they name: `dest_group`: among the 128 blocks of one device at most 16 name the same target group, and in every draw some device has exactly 16 blocks to one group.
All inputs are finite; a program needn't handle non-finite values.
Results may differ from the reference program's by a relative error of at most 0.0018.
Values may be sent and summed in bfloat16 or wider, within the bound.
No kernel may reach another device: no remote copies, remote signals or barrier semaphores. Data moves between devices by JAX's collectives and lax.ppermute only.
A program may use at most 128 MiB of HBM per device.

```python
import math
import jax
import jax.numpy as jnp
import numpy as np
from jax import lax

CL = 256
R = 64
RHS = 32
CLU_DEV = 2
BLK_DEV = 128
NEAR_DEV = 4
CAP = 16
NPTS = 65536
NBLK = 32768
USLOTS = 65536
NNEAR = 1024
N_COMP = 2
N_TGT = 16
N_SRC = 8


def touch_ends(drawn, key, least, largest):
    longest = drawn.shape.index(max(drawn.shape))
    spots = []
    for shift in (0, 1):
        where = [jax.random.randint(jax.random.fold_in(key, axis), (), 0, length) for axis, length in enumerate(drawn.shape)]
        where[longest] = (where[longest] + shift) % drawn.shape[longest]
        spots.append(tuple(where))
    return drawn.at[spots[0]].set(least).at[spots[1]].set(largest)


def steps_of(own_key, dims, shards, smallest, largest):
    level = 1.0
    for axis_at, shards_of in shards:
        steps = jax.random.uniform(jax.random.fold_in(jax.random.fold_in(own_key, 6), axis_at), (shards_of,), jnp.float32, smallest / len(shards), largest / len(shards))
        level = level * jnp.repeat(jnp.exp(steps), dims[axis_at] // shards_of).reshape((-1,) + (1,) * (len(dims) - 1 - axis_at))
    return level


def assign_block(own_key, own, number, rows, count, top, reach, skew):
    order = jax.random.permutation(own_key, count)
    crowded, usual = load_shares(count, rows * top, reach, skew, True), load_shares(count, rows * top, reach, skew, False)
    places = jnp.arange(count)

    def named(sizes, offset_by):
        used = int((sizes > 0).sum())
        fixed = max(1, used // 4)
        shifted = fixed + (places - fixed + offset_by * (used - fixed)) % max(1, count - fixed)
        return jnp.zeros((count,), jnp.int32).at[order[jnp.where(places < fixed, places, shifted)]].set(jnp.asarray(sizes, jnp.int32))

    sizes = jnp.where(number % 4 == 0, named(crowded, number // 4), named(usual, number - number // 4 - 1))
    mixed = jax.random.permutation(jax.random.fold_in(own, 3), count)
    donor, taker = mixed[0:count // 2 * 2:2], mixed[1:count // 2 * 2:2]
    room = jnp.minimum(sizes[donor] - 1, reach - sizes[taker]) // 2
    room = jnp.where((donor == order[0]) | (taker == order[0]) | (sizes[taker] == 0), 0, jnp.maximum(room, 0))
    shifted = jax.random.randint(jax.random.fold_in(own, 4), (count // 2,), 0, 1 << 20) % (room + 1)
    sizes = sizes.at[donor].add(-shifted).at[taker].add(shifted)
    members = jnp.searchsorted(jnp.cumsum(sizes), jnp.arange(rows * top), side="right").astype(jnp.int32)
    grid = members.reshape(top, rows).T
    grid = grid[jax.random.permutation(jax.random.fold_in(own, 1), rows)]
    offset_by = jax.random.randint(jax.random.fold_in(own, 2), (rows, 1), 0, top)
    return jnp.take_along_axis(grid, (jnp.arange(top)[None, :] + offset_by) % top, axis=1)


def load_shares(count, total, most, lean, full):
    portions = [(1 << 20) // math.isqrt(standing ** lean) + 1 for standing in range(1, count + 1)]
    largest = most if full else min(most, max(-(-total // count), total * portions[0] // sum(portions)))
    least = 1 if total - largest >= count - 1 else 0
    counts, surplus = [largest] + [least] * (count - 1), total - largest - least * (count - 1)
    while surplus > 0:
        candidates = [i for i in range(1, count) if counts[i] < largest] or [i for i in range(1, count) if counts[i] < most]
        whole, left = sum([portions[i] for i in candidates]), surplus
        for i in candidates:
            addition = min(most - counts[i], max(1, left * portions[i] // whole), surplus)
            counts[i] = counts[i] + addition
            surplus = surplus - addition
    return np.array(counts)


def noise(own_key, extent, scale, reach, shards=(), kind=jnp.bfloat16):
    loudness = steps_of(own_key, extent, shards, -0.22, 0.18) if shards else 1.0
    values = jax.random.normal(own_key, extent, jnp.float32) * scale * loudness
    return jnp.minimum(jnp.maximum(values, -reach), reach).astype(kind)


def setup_inputs(seed: int = 0) -> dict:
    streams_of = jax.random.split(jax.random.key(seed), 13)
    field = noise(streams_of[0], (3, RHS, NPTS), 1.0, 6.0, ((2, 128),))
    dest_group_keys = jax.random.split(jax.random.fold_in(streams_of[1], 1), NBLK // BLK_DEV)
    dest_group_turns = jax.random.permutation(jax.random.fold_in(streams_of[1], 3), NBLK // BLK_DEV)
    dest_group = jax.vmap(lambda own, number: assign_block(jax.random.fold_in(streams_of[1], 2), own, number, BLK_DEV, N_TGT, 1, CAP, 2))(dest_group_keys, dest_group_turns).reshape((NBLK, 1))
    src_local = touch_ends(jax.random.randint(streams_of[2], (NBLK,), 0, CLU_DEV), jax.random.fold_in(streams_of[2], 1), 0, CLU_DEV - 1).astype(jnp.int32)
    ranks = touch_ends(jax.random.randint(streams_of[3], (NBLK,), max(1, R // 8), R + 1), jax.random.fold_in(streams_of[3], 1), max(1, R // 8), R).astype(jnp.int32)
    mixing = noise(streams_of[4], (NBLK, 3, 3), 1.0, 5.0, ((0, 256),), jnp.float32)
    v_factor = noise(streams_of[5], (NBLK, R, CL), CL ** -0.5, 0.375, ((0, 256),))
    u_factor = noise(streams_of[6], (USLOTS, R, CL), (R * BLK_DEV) ** -0.5, 0.0625, ((0, 256),))
    slot_cluster = touch_ends(jax.random.randint(streams_of[7], (USLOTS,), 0, CLU_DEV * N_SRC), jax.random.fold_in(streams_of[7], 1), 0, (CLU_DEV * N_SRC) - 1).astype(jnp.int32)
    near_src = touch_ends(jax.random.randint(streams_of[8], (NNEAR,), 0, CLU_DEV), jax.random.fold_in(streams_of[8], 1), 0, CLU_DEV - 1).astype(jnp.int32)
    near_tgt = touch_ends(jax.random.randint(streams_of[9], (NNEAR,), 0, CLU_DEV * N_SRC), jax.random.fold_in(streams_of[9], 1), 0, (CLU_DEV * N_SRC) - 1).astype(jnp.int32)
    near_mixing = noise(streams_of[10], (NNEAR, 3, 3), 1.0, 5.0, ((0, 256),), jnp.float32)
    near_matrix = noise(streams_of[11], (NNEAR, CL, CL), (CL * NEAR_DEV) ** -0.5, 0.1875, ((0, 256),))
    return dict(field=field, dest_group=dest_group, src_local=src_local, ranks=ranks, mixing=mixing, v_factor=v_factor, u_factor=u_factor, slot_cluster=slot_cluster, near_src=near_src, near_tgt=near_tgt, near_mixing=near_mixing, near_matrix=near_matrix)


def reference(field, dest_group, src_local, ranks, mixing, v_factor, u_factor, slot_cluster, near_src, near_tgt, near_mixing, near_matrix):
    devices = N_COMP * N_TGT * N_SRC
    channels = 3 * RHS
    half_owned = CLU_DEV // 2
    source_count = N_TGT * N_SRC * CLU_DEV
    sources = jnp.transpose(field.reshape(channels, source_count, CL), (1, 0, 2))
    device_ids = jnp.arange(devices, dtype=jnp.int32)
    comp_of = device_ids // (N_TGT * N_SRC)
    tgt_of = (device_ids // N_SRC) % N_TGT
    src_of = device_ids % N_SRC
    destination = dest_group.reshape(devices, BLK_DEV).astype(jnp.int32)
    member = (destination[:, :, None] == jnp.arange(N_TGT, dtype=jnp.int32)[None, None, :]).astype(jnp.int32)
    position = jnp.sum(jnp.cumsum(member, axis=1) * member, axis=2) - 1
    sender_row = tgt_of * N_SRC + src_of
    source_ids = sender_row[:, None] * CLU_DEV + src_local.reshape(devices, BLK_DEV)
    receiver = (comp_of[:, None] * N_TGT + destination) * N_SRC + src_of[:, None]
    u_rows = (receiver * (N_TGT * CAP) + tgt_of[:, None] * CAP + position).astype(jnp.int32)
    within = slot_cluster[u_rows.reshape(-1)].reshape(devices, BLK_DEV)

    def global_target(group, inner):
        comp_part = inner // (N_SRC * half_owned)
        src_part = (inner // half_owned) % N_SRC
        local_part = inner % half_owned
        return (((comp_part * N_TGT + group) * N_SRC + src_part) * half_owned + local_part).astype(jnp.int32)

    far_targets = global_target(destination, within)
    near_targets = global_target(jnp.broadcast_to(tgt_of[:, None], (devices, NEAR_DEV)), near_tgt.reshape(devices, NEAR_DEV))
    near_sources = sender_row[:, None] * CLU_DEV + near_src.reshape(devices, NEAR_DEV)
    total = jnp.zeros((N_COMP * N_TGT * N_SRC * half_owned, channels, CL), jnp.float32)

    def far_step(carry, items):
        source_rows, rank_row, mix_row, v_rows, u_index, target_rows = items
        inputs = sources[source_rows].astype(jnp.float32)
        coefficients = jnp.einsum("bfp,brp->bfr", inputs, v_rows.astype(jnp.float32))
        rank_mask = (jnp.arange(R, dtype=jnp.int32)[None, :] < rank_row[:, None]).astype(jnp.float32)
        coefficients = (coefficients * rank_mask[:, None, :]).reshape(BLK_DEV, 3, RHS, R)
        mixed_coef = jnp.einsum("bcd,bdsr->bcsr", mix_row.astype(jnp.float32), coefficients)
        sent = lax.optimization_barrier(mixed_coef.reshape(BLK_DEV, channels, R).astype(jnp.bfloat16))
        basis = u_factor[u_index].astype(jnp.float32)
        contrib = jnp.einsum("bfr,brq->bfq", sent.astype(jnp.float32), basis)
        return carry.at[target_rows].add(contrib), None

    total, unused = lax.scan(far_step, total, (source_ids, ranks.reshape(devices, BLK_DEV), mixing.reshape(devices, BLK_DEV, 3, 3), v_factor.reshape(devices, BLK_DEV, R, CL), u_rows, far_targets))

    def near_step(carry, items):
        source_rows, mix_row, dense_rows, target_rows = items
        inputs = sources[source_rows].astype(jnp.float32)
        dense_out = jnp.einsum("nfp,nqp->nfq", inputs, dense_rows.astype(jnp.float32)).reshape(NEAR_DEV, 3, RHS, CL)
        mixed_near = jnp.einsum("ncd,ndsq->ncsq", mix_row.astype(jnp.float32), dense_out).reshape(NEAR_DEV, channels, CL)
        return carry.at[target_rows].add(mixed_near), None

    total, unused = lax.scan(near_step, total, (near_sources, near_mixing.reshape(devices, NEAR_DEV, 3, 3), near_matrix.reshape(devices, NEAR_DEV, CL, CL), near_targets))
    return jnp.transpose(total, (1, 0, 2)).reshape(3, RHS, NPTS)
```

```python
import functools

import jax
import jax.numpy as jnp
from jax import lax
from jax.experimental import pallas as pl
from jax.experimental.pallas import tpu as pltpu
from jax.sharding import PartitionSpec as P

SUB = 8
QUAD = 4


def spread(values, lane, width):
    out = values[-1]
    for t in range(len(values) - 2, -1, -1):
        out = jnp.where(lane < (t + 1) * width, values[t], out)
    return out


def source_kernel(
    comps, groups, capacity, dest, src, ranks, mixing, field, v, out, x, slots, counts
):
    step = pl.program_id(0)
    per_step = out.shape[0]
    blocks, rank_width, cluster = v.shape
    channels = out.shape[1]
    rhs = channels // comps
    owned = x.shape[0] // channels

    @pl.when(step == 0)
    def _():
        for s in range(owned):
            x[s * channels : (s + 1) * channels, :] = field[:, s * cluster : (s + 1) * cluster]
        for g in range(groups):
            counts[g] = 0

        def place(b, carry):
            g = dest[b]
            k = counts[g]
            counts[g] = k + 1
            slots[g * capacity + k] = b
            return carry

        lax.fori_loop(0, blocks, place, 0, unroll=8)

    width = QUAD * rank_width
    lane = lax.broadcasted_iota(jnp.int32, (SUB, width), 1)
    within = lane & (rank_width - 1)

    def one_group(n, carry):
        g = step * per_step + n
        count = counts[g]
        for q in range(capacity // QUAD):
            cols = slice(q * width, (q + 1) * width)

            @pl.when(count > q * QUAD)
            def _():
                first = g * capacity + q * QUAD
                full = [count > q * QUAD + t for t in range(QUAD)]
                ids = [jnp.where(full[t], slots[first + t], 0) for t in range(QUAD)]
                basis = jnp.concatenate([v[b] for b in ids], axis=0)
                y = lax.dot_general(
                    x[...], basis, (((1,), (1,)), ((), ())), preferred_element_type=jnp.float32
                ).reshape(owned, comps, rhs // SUB, SUB, width)
                which = spread([src[b] for b in ids], lane, rank_width)
                picked = y[0]
                for s in range(1, owned):
                    picked = jnp.where(which == s, y[s], picked)
                limit = spread(
                    [jnp.where(full[t], ranks[ids[t]], 0) for t in range(QUAD)], lane, rank_width
                )
                kept = within < limit
                for e in range(comps):
                    total = None
                    for e2 in range(comps):
                        entry = (e * comps + e2) * blocks
                        m = spread([mixing[entry + b] for b in ids], lane, rank_width)
                        m = jnp.where(kept, m, 0.0)
                        term = m * picked[e2]
                        total = term if total is None else total + term
                    out[n, e * rhs : (e + 1) * rhs, cols] = total.reshape(rhs, width).astype(
                        out.dtype
                    )

            @pl.when(count <= q * QUAD)
            def _():
                out[n, :, cols] = jnp.zeros((channels, width), out.dtype)

        return carry

    lax.fori_loop(0, per_step, one_group, 0)


def target_kernel(
    comps, place, slot_cluster, near_src, near_tgt, near_mixing, where, field, near, u, sent, mine, other
):
    step = pl.program_id(0)
    per_step, channels, lanes = sent.shape
    slot_rows, rank_width, cluster = u.shape
    capacity = slot_rows // per_step
    width = QUAD * rank_width
    near_count = near.shape[0]
    rhs = channels // comps
    core = where[0]

    def add(w, value):
        row, own = place(w, core)

        @pl.when(own)
        def _():
            mine[row] += value

        @pl.when(jnp.logical_not(own))
        def _():
            other[row] += value

    @pl.when(step == 0)
    def _():
        mine[...] = jnp.zeros_like(mine)
        other[...] = jnp.zeros_like(other)
        for n in range(near_count):
            begin = pl.multiple_of(near_src[n] * cluster, cluster)
            y = lax.dot_general(
                field[:, pl.ds(begin, cluster)],
                near[n],
                (((1,), (1,)), ((), ())),
                preferred_element_type=jnp.float32,
            )
            parts = [y[e * rhs : (e + 1) * rhs] for e in range(comps)]
            rows = []
            for e in range(comps):
                total = None
                for e2 in range(comps):
                    term = near_mixing[(e * comps + e2) * near_count + n] * parts[e2]
                    total = term if total is None else total + term
                rows.append(total)
            add(near_tgt[n], jnp.concatenate(rows, axis=0))

    lane = lax.broadcasted_iota(jnp.int32, (1, width), 1)
    for n in range(per_step):
        for q in range(capacity // QUAD):
            a = sent[n, :, q * width : (q + 1) * width]
            first = n * capacity + q * QUAD
            basis = u[first : first + QUAD].reshape(width, cluster)
            for t in range(QUAD):
                inside = (lane >= t * rank_width) & (lane < (t + 1) * rank_width)
                one = jnp.where(inside, a, jnp.zeros_like(a))
                far = jnp.dot(one, basis, preferred_element_type=jnp.float32)
                add(slot_cluster[step * slot_rows + first + t], far)


def body(
    field,
    dest_group,
    src_local,
    ranks,
    mixing,
    v_factor,
    u_factor,
    slot_cluster,
    near_src,
    near_tgt,
    near_mixing,
    near_matrix,
):
    groups = lax.axis_size("tgt")
    shards = lax.axis_size("src")
    pairing = lax.axis_size("comp")
    blocks, rank_width, cluster = v_factor.shape
    comps, vectors, points = field.shape
    channels = comps * vectors
    owned = points // cluster
    slot_count = u_factor.shape[0]
    capacity = slot_count // groups
    near_count = near_matrix.shape[0]
    cores = 2
    chips = pairing * shards // cores
    smem = pl.BlockSpec(memory_space=pltpu.SMEM)

    x = field.reshape(channels, points)
    per_step = 4
    outgoing = pl.pallas_call(
        functools.partial(source_kernel, comps, groups, capacity),
        grid=(groups // per_step,),
        out_shape=jax.ShapeDtypeStruct((groups, channels, capacity * rank_width), jnp.bfloat16),
        in_specs=[smem] * 4
        + [
            pl.BlockSpec((channels, points), lambda i: (0, 0)),
            pl.BlockSpec(v_factor.shape, lambda i: (0, 0, 0), pipeline_mode=pl.Buffered(1)),
        ],
        out_specs=pl.BlockSpec((per_step, channels, capacity * rank_width), lambda i: (i, 0, 0)),
        scratch_shapes=[
            pltpu.VMEM((owned * channels, cluster), jnp.bfloat16),
            pltpu.SMEM((slot_count,), jnp.int32),
            pltpu.SMEM((groups,), jnp.int32),
        ],
        compiler_params=pltpu.CompilerParams(vmem_limit_bytes=48 << 20),
        name="source",
    )(
        dest_group[:, 0],
        src_local,
        ranks,
        mixing.transpose(1, 2, 0).reshape(-1),
        x,
        v_factor,
    )
    incoming = lax.all_to_all(outgoing, "tgt", split_axis=0, concat_axis=0, tiled=True)

    def place(w, core):
        c, j = w // shards, w % shards
        return (j // cores) * pairing + c, (j % cores) == core

    core = (lax.axis_index("src") % cores).astype(jnp.int32).reshape(1)
    steps = 8
    senders = groups // steps
    half = jax.ShapeDtypeStruct((chips, channels, cluster), jnp.float32)
    whole = pl.BlockSpec(half.shape, lambda i: (0, 0, 0))
    mine, other = pl.pallas_call(
        functools.partial(target_kernel, comps, place),
        grid=(steps,),
        out_shape=[half, half],
        in_specs=[smem] * 5
        + [
            pl.BlockSpec((channels, points), lambda i: (0, 0)),
            pl.BlockSpec(near_matrix.shape, lambda i: (0, 0, 0)),
            pl.BlockSpec((senders * capacity, rank_width, cluster), lambda i: (i, 0, 0)),
            pl.BlockSpec((senders, channels, capacity * rank_width), lambda i: (i, 0, 0)),
        ],
        out_specs=[whole, whole],
        compiler_params=pltpu.CompilerParams(vmem_limit_bytes=48 << 20),
        name="target",
    )(
        slot_cluster,
        near_src,
        near_tgt,
        near_mixing.transpose(1, 2, 0).reshape(-1),
        core,
        x,
        near_matrix,
        u_factor,
        incoming,
    )
    swapped = lax.ppermute(other, "src", [(j, j ^ 1) for j in range(shards)])
    sums = (mine + swapped).astype(jnp.bfloat16)
    lines = [
        [c * shards + h * cores + k for h in range(shards // cores) for c in range(pairing)]
        for k in range(cores)
    ]
    parts = lax.all_to_all(
        sums, ("comp", "src"), split_axis=0, concat_axis=0, tiled=True, axis_index_groups=lines
    )
    return parts.astype(jnp.float32).sum(axis=0).reshape(comps, vectors, cluster)


def solution(mesh):
    every = ("comp", "tgt", "src")
    placed = (
        P(None, None, ("tgt", "src")),
        P(every, None),
        P(every),
        P(every),
        P(every, None, None),
        P(every, None, None),
        P(every, None, None),
        P(every),
        P(every),
        P(every),
        P(every, None, None),
        P(every, None, None),
    )
    return jax.shard_map(
        body,
        mesh=mesh,
        in_specs=placed,
        out_specs=P(None, None, every),
        check_vma=False,
    )
```

```python
import functools

import jax
import jax.numpy as jnp
from jax import lax
from jax.experimental import pallas as pl
from jax.experimental.pallas import tpu as pltpu
from jax.sharding import PartitionSpec as P

SUB = 8
QUAD = 4


def spread(values, lane, width):
    out = values[-1]
    for t in range(len(values) - 2, -1, -1):
        out = jnp.where(lane < (t + 1) * width, values[t], out)
    return out


def source_kernel(
    comps,
    dest_hbm,
    src_hbm,
    ranks_hbm,
    mixing_hbm,
    field_hbm,
    v_hbm,
    out,
    dest,
    src,
    ranks,
    mixing,
    field,
    v,
    x,
    slots,
    counts,
    small_sem,
    big_sem,
):
    step = pl.program_id(0)
    per_step = out.shape[0]
    blocks, rank_width, cluster = v.shape
    channels = out.shape[1]
    rhs = channels // comps
    owned = x.shape[0] // channels
    groups = counts.shape[0]
    capacity = slots.shape[0] // groups

    @pl.when(step == 0)
    def _():
        small = [
            pltpu.make_async_copy(a, b, small_sem.at[n])
            for n, (a, b) in enumerate(
                ((dest_hbm, dest), (src_hbm, src), (ranks_hbm, ranks), (field_hbm, field))
            )
        ]
        small += [
            pltpu.make_async_copy(
                mixing_hbm.at[e, e2], mixing.at[e * comps + e2], small_sem.at[4 + e * comps + e2]
            )
            for e in range(comps)
            for e2 in range(comps)
        ]
        big = pltpu.make_async_copy(v_hbm, v, big_sem)
        for copy in small:
            copy.start()
        big.start()
        for g in range(groups):
            counts[g] = 0
        for copy in small:
            copy.wait()
        for s in range(owned):
            x[s * channels : (s + 1) * channels, :] = field[:, s * cluster : (s + 1) * cluster]

        def put(b, carry):
            g = dest[b]
            k = counts[g]
            counts[g] = k + 1
            slots[g * capacity + k] = b
            return carry

        lax.fori_loop(0, blocks, put, 0, unroll=8)
        big.wait()

    width = QUAD * rank_width
    lane = lax.broadcasted_iota(jnp.int32, (SUB, width), 1)
    within = lane & (rank_width - 1)

    def one_group(n, carry):
        g = step * per_step + n
        count = counts[g]
        for q in range(capacity // QUAD):
            cols = slice(q * width, (q + 1) * width)
            first = g * capacity + q * QUAD
            full = [count > q * QUAD + t for t in range(QUAD)]
            ids = [jnp.where(full[t], slots[first + t], 0) for t in range(QUAD)]
            basis = jnp.concatenate([v[b] for b in ids], axis=0)
            y = lax.dot_general(
                x[...], basis, (((1,), (1,)), ((), ())), preferred_element_type=jnp.float32
            ).reshape(owned, comps, rhs // SUB, SUB, width)
            which = spread([src[b] for b in ids], lane, rank_width)
            picked = y[0]
            for s in range(1, owned):
                picked = jnp.where(which == s, y[s], picked)
            limit = spread(
                [jnp.where(full[t], ranks[ids[t]], 0) for t in range(QUAD)], lane, rank_width
            )
            kept = within < limit
            for e in range(comps):
                total = None
                for e2 in range(comps):
                    m = spread([mixing[e * comps + e2, b] for b in ids], lane, rank_width)
                    m = jnp.where(kept, m, 0.0)
                    term = m * picked[e2]
                    total = term if total is None else total + term
                out[n, e * rhs : (e + 1) * rhs, cols] = total.reshape(rhs, width).astype(out.dtype)
        return carry

    lax.fori_loop(0, per_step, one_group, 0)


def target_kernel(
    comps,
    place,
    clusters_hbm,
    near_src_hbm,
    near_tgt_hbm,
    near_mixing_hbm,
    field_hbm,
    near_hbm,
    u,
    sent,
    mine,
    other,
    clusters,
    near_src,
    near_tgt,
    near_mixing,
    field,
    near,
    total_by_row,
    sems,
):
    step = pl.program_id(0)
    per_step, channels, lanes = sent.shape
    slot_rows, rank_width, cluster = u.shape
    capacity = slot_rows // per_step
    width = QUAD * rank_width
    near_count = near.shape[0]
    rhs = channels // comps
    rows = mine.shape[0]

    def add(w, value):
        row, own = place(w)
        total_by_row[jnp.where(own, row, row + rows)] += value

    @pl.when(step == 0)
    def _():
        copies = [
            pltpu.make_async_copy(a, b, sems.at[n])
            for n, (a, b) in enumerate(
                (
                    (clusters_hbm, clusters),
                    (near_src_hbm, near_src),
                    (near_tgt_hbm, near_tgt),
                    (near_mixing_hbm, near_mixing),
                    (field_hbm, field),
                    (near_hbm, near),
                )
            )
        ]
        for copy in copies:
            copy.start()
        total_by_row[...] = jnp.zeros_like(total_by_row)
        for copy in copies:
            copy.wait()
        for n in range(near_count):
            begin = pl.multiple_of(near_src[n] * cluster, cluster)
            y = lax.dot_general(
                field[:, pl.ds(begin, cluster)],
                near[n],
                (((1,), (1,)), ((), ())),
                preferred_element_type=jnp.float32,
            )
            parts = [y[e * rhs : (e + 1) * rhs] for e in range(comps)]
            mixed = []
            for e in range(comps):
                total = None
                for e2 in range(comps):
                    term = near_mixing[e, n : n + 1, e2 : e2 + 1] * parts[e2]
                    total = term if total is None else total + term
                mixed.append(total)
            add(near_tgt[n], jnp.concatenate(mixed, axis=0))

    lane = lax.broadcasted_iota(jnp.int32, (1, width), 1)
    inside = [(lane >= t * rank_width) & (lane < (t + 1) * rank_width) for t in range(QUAD)]
    for n in range(per_step):
        for q in range(capacity // QUAD):
            a = sent[n, :, q * width : (q + 1) * width]
            first = n * capacity + q * QUAD
            basis = u[first : first + QUAD].reshape(width, cluster)
            one = jnp.concatenate([jnp.where(m, a, jnp.zeros_like(a)) for m in inside], axis=0)
            far = jnp.dot(one, basis, preferred_element_type=jnp.float32)
            for t in range(QUAD):
                add(
                    clusters[step * slot_rows + first + t],
                    far[t * channels : (t + 1) * channels],
                )

    @pl.when(step == pl.num_programs(0) - 1)
    def _():
        mine[...] = total_by_row[:rows]
        other[...] = total_by_row[rows:]


def body(
    field,
    dest_group,
    src_local,
    ranks,
    mixing,
    v_factor,
    u_factor,
    slot_cluster,
    near_src,
    near_tgt,
    near_mixing,
    near_matrix,
):
    groups = lax.axis_size("tgt")
    shards = lax.axis_size("src")
    pairing = lax.axis_size("comp")
    blocks, rank_width, cluster = v_factor.shape
    comps, vectors, points = field.shape
    channels = comps * vectors
    owned = points // cluster
    slot_count = u_factor.shape[0]
    capacity = slot_count // groups
    near_count = near_matrix.shape[0]
    cores = 2
    chips = pairing * shards // cores
    kept = functools.partial(pltpu.with_memory_space_constraint, memory_space=pltpu.HBM)
    hbm = pl.BlockSpec(memory_space=pltpu.HBM)

    x = kept(field.reshape(channels, points))
    per_step = 4
    outgoing = pl.pallas_call(
        functools.partial(source_kernel, comps),
        grid=(groups // per_step,),
        out_shape=jax.ShapeDtypeStruct((groups, channels, capacity * rank_width), jnp.bfloat16),
        in_specs=[hbm] * 6,
        out_specs=pl.BlockSpec((per_step, channels, capacity * rank_width), lambda i: (i, 0, 0)),
        scratch_shapes=[
            pltpu.SMEM((blocks,), jnp.int32),
            pltpu.SMEM((blocks,), jnp.int32),
            pltpu.SMEM((blocks,), jnp.int32),
            pltpu.SMEM((comps * comps, blocks), jnp.float32),
            pltpu.VMEM((channels, points), jnp.bfloat16),
            pltpu.VMEM(v_factor.shape, jnp.bfloat16),
            pltpu.VMEM((owned * channels, cluster), jnp.bfloat16),
            pltpu.SMEM((slot_count,), jnp.int32),
            pltpu.SMEM((groups,), jnp.int32),
            pltpu.SemaphoreType.DMA((4 + comps * comps,)),
            pltpu.SemaphoreType.DMA,
        ],
        compiler_params=pltpu.CompilerParams(vmem_limit_bytes=48 << 20),
        name="source",
    )(
        kept(dest_group[:, 0]),
        kept(src_local),
        kept(ranks),
        kept(mixing.transpose(1, 2, 0)),
        x,
        kept(v_factor),
    )
    incoming = lax.all_to_all(outgoing, "tgt", split_axis=0, concat_axis=0, tiled=True)

    def place(w):
        c, j = w // shards, w % shards
        core = lax.rem(lax.axis_index("src"), cores)
        return (j // cores) * pairing + c, (j % cores) == core

    steps = 8
    senders = groups // steps
    half = jax.ShapeDtypeStruct((chips, channels, cluster), jnp.float32)
    whole = pl.BlockSpec(half.shape, lambda i: (0, 0, 0))
    mine, other = pl.pallas_call(
        functools.partial(target_kernel, comps, place),
        grid=(steps,),
        out_shape=[half, half],
        in_specs=[hbm] * 6
        + [
            pl.BlockSpec((senders * capacity, rank_width, cluster), lambda i: (i, 0, 0)),
            pl.BlockSpec((senders, channels, capacity * rank_width), lambda i: (i, 0, 0)),
        ],
        out_specs=[whole, whole],
        scratch_shapes=[
            pltpu.SMEM((slot_count,), jnp.int32),
            pltpu.SMEM((near_count,), jnp.int32),
            pltpu.SMEM((near_count,), jnp.int32),
            pltpu.VMEM((comps, near_count, comps), jnp.float32),
            pltpu.VMEM((channels, points), jnp.bfloat16),
            pltpu.VMEM(near_matrix.shape, jnp.bfloat16),
            pltpu.VMEM((2 * chips, channels, cluster), jnp.float32),
            pltpu.SemaphoreType.DMA((6,)),
        ],
        compiler_params=pltpu.CompilerParams(vmem_limit_bytes=48 << 20),
        name="target",
    )(
        kept(slot_cluster),
        kept(near_src),
        kept(near_tgt),
        kept(near_mixing.transpose(1, 0, 2)),
        x,
        kept(near_matrix),
        kept(u_factor),
        incoming,
    )
    swapped = lax.ppermute(other, "src", [(j, j ^ 1) for j in range(shards)])
    sums = mine + swapped
    lines = [
        [c * shards + h * cores + k for h in range(shards // cores) for c in range(pairing)]
        for k in range(cores)
    ]
    parts = lax.all_to_all(
        sums.astype(jnp.bfloat16),
        ("comp", "src"),
        split_axis=0,
        concat_axis=0,
        tiled=True,
        axis_index_groups=lines,
    )
    row = (lax.axis_index("src") // cores) * pairing + lax.axis_index("comp")
    own = (jnp.arange(chips, dtype=jnp.int32) == row)[:, None, None]
    result = jnp.where(own, sums, parts.astype(jnp.float32)).sum(axis=0)
    return result.reshape(comps, vectors, cluster)


def solution(mesh):
    every = ("comp", "tgt", "src")
    placed = (
        P(None, None, ("tgt", "src")),
        P(every, None),
        P(every),
        P(every),
        P(every, None, None),
        P(every, None, None),
        P(every, None, None),
        P(every),
        P(every),
        P(every),
        P(every, None, None),
        P(every, None, None),
    )
    return jax.shard_map(
        body,
        mesh=mesh,
        in_specs=placed,
        out_specs=P(None, None, every),
        check_vma=False,
    )
```

```python
import functools

import jax
import jax.numpy as jnp
from jax import lax
from jax.experimental import pallas as pl
from jax.experimental.pallas import tpu as pltpu
from jax.sharding import PartitionSpec as P

SUB = 8
QUAD = 4
TOGETHER = 8
PIECES = 4
UNROLL = 4
SOURCE_MIB = 20
TARGET_MIB = 20


def pieces(length):
    size = length // PIECES
    return [pl.ds(n * size, size) for n in range(PIECES)]


def spread(values, lane, width):
    out = values[-1]
    for t in range(len(values) - 2, -1, -1):
        out = jnp.where(lane < (t + 1) * width, values[t], out)
    return out


def source_kernel(
    comps,
    place,
    dest_hbm,
    src_hbm,
    ranks_hbm,
    mixing_hbm,
    near_src_hbm,
    near_tgt_hbm,
    near_mixing_hbm,
    field_hbm,
    near_hbm,
    v_hbm,
    u_hbm,
    out,
    u,
    table,
    dest,
    src,
    ranks,
    mixing,
    near_src,
    near_tgt,
    near_mixing,
    field,
    near,
    v,
    x,
    slots,
    sets,
    counts,
    small_sems,
    big_sems,
):
    blocks, rank_width, cluster = v.shape
    groups, channels, lanes = out.shape
    rhs = channels // comps
    owned = x.shape[0] // channels
    capacity = slots.shape[0] // groups
    near_count = near.shape[0]

    pairs = [
        (dest_hbm, dest),
        (src_hbm, src),
        (ranks_hbm, ranks),
        (near_src_hbm, near_src),
        (near_tgt_hbm, near_tgt),
        (near_mixing_hbm, near_mixing),
        (field_hbm, field),
    ] + [
        (mixing_hbm.at[e, e2], mixing.at[e * comps + e2]) for e in range(comps) for e2 in range(comps)
    ]
    small = [pltpu.make_async_copy(p, q, small_sems.at[n]) for n, (p, q) in enumerate(pairs)]
    big = [
        pltpu.make_async_copy(p, q, big_sems.at[n])
        for n, (p, q) in enumerate(
            [(near_hbm, near)]
            + [(v_hbm.at[piece], v.at[piece]) for piece in pieces(blocks)]
            + [(u_hbm.at[piece], u.at[piece]) for piece in pieces(slots.shape[0])]
        )
    ]
    for copy in small + big[: 1 + PIECES]:
        copy.start()
    table[...] = jnp.zeros_like(table)
    out[...] = jnp.zeros_like(out)
    for g in range(groups):
        counts[g] = 0
    for copy in small:
        copy.wait()

    def put(b, carry):
        g = dest[b]
        k = counts[g]
        counts[g] = k + 1
        slots[g * capacity + k] = b
        return carry

    lax.fori_loop(0, blocks, put, 0, unroll=8)
    used = jnp.int32(0)
    for g in range(groups):
        for q in range(capacity // QUAD):
            sets[used] = g * (capacity // QUAD) + q
            used = used + (counts[g] > q * QUAD).astype(jnp.int32)
    for n in range(TOGETHER):
        sets[used + n] = sets[0]
    for s in range(owned):
        x[s * channels : (s + 1) * channels, :] = field[:, s * cluster : (s + 1) * cluster]
    big[0].wait()
    for n in range(near_count):
        begin = pl.multiple_of(near_src[n] * channels, channels)
        y = lax.dot_general(
            x[pl.ds(begin, channels), :],
            near[n],
            (((1,), (1,)), ((), ())),
            preferred_element_type=jnp.float32,
        )
        parts = [y[e * rhs : (e + 1) * rhs] for e in range(comps)]
        row = place(near_tgt[n])
        for e in range(comps):
            total = None
            for e2 in range(comps):
                term = near_mixing[e, n : n + 1, e2 : e2 + 1] * parts[e2]
                total = term if total is None else total + term
            table[row, e * rhs : (e + 1) * rhs, :] += total
    for copy in big[1 : 1 + PIECES]:
        copy.wait()
    for copy in big[1 + PIECES :]:
        copy.start()

    width = QUAD * rank_width
    lane = lax.broadcasted_iota(jnp.int32, (SUB, width), 1)
    within = lane & (rank_width - 1)

    def one_set(number):
        g = lax.div(number, capacity // QUAD)
        begin = lax.rem(number, capacity // QUAD) * QUAD
        count = counts[g]
        first = number * QUAD
        full = [count > begin + t for t in range(QUAD)]
        ids = [jnp.where(full[t], slots[first + t], 0) for t in range(QUAD)]
        basis = jnp.concatenate([v[b] for b in ids], axis=0)
        y = lax.dot_general(
            x[...], basis, (((1,), (1,)), ((), ())), preferred_element_type=jnp.float32
        ).reshape(owned, comps, rhs // SUB, SUB, width)
        which = spread([src[b] for b in ids], lane, rank_width)
        picked = y[0]
        for s in range(1, owned):
            picked = jnp.where(which == s, y[s], picked)
        limit = spread(
            [jnp.where(full[t], ranks[ids[t]], 0) for t in range(QUAD)], lane, rank_width
        )
        kept = within < limit
        cols = pl.ds(pl.multiple_of(begin * rank_width, width), width)
        for e in range(comps):
            total = None
            for e2 in range(comps):
                m = spread([mixing[e * comps + e2, b] for b in ids], lane, rank_width)
                m = jnp.where(kept, m, 0.0)
                term = m * picked[e2]
                total = term if total is None else total + term
            out[g, e * rhs : (e + 1) * rhs, cols] = total.reshape(rhs, width).astype(out.dtype)

    def one_pass(n, carry):
        for m in range(TOGETHER):
            one_set(sets[n * TOGETHER + m])
        return carry

    lax.fori_loop(0, lax.div(used + TOGETHER - 1, TOGETHER), one_pass, 0)
    for copy in big[1 + PIECES :]:
        copy.wait()


def target_kernel(place, clusters_hbm, u, sent, near_table, table, other, clusters, sem):
    senders, channels, lanes = sent.shape
    slot_count, rank_width, cluster = u.shape
    capacity = slot_count // senders
    width = QUAD * rank_width
    copy = pltpu.make_async_copy(clusters_hbm, clusters, sem)
    copy.start()
    lane = lax.broadcasted_iota(jnp.int32, (1, width), 1)
    inside = [(lane >= t * rank_width) & (lane < (t + 1) * rank_width) for t in range(QUAD)]
    copy.wait()

    def one_sender(i, carry):
        for q in range(capacity // QUAD):
            a = sent[i, :, q * width : (q + 1) * width]
            first = i * capacity + q * QUAD
            basis = u[pl.ds(first, QUAD)].reshape(width, cluster)
            one = jnp.concatenate([jnp.where(m, a, jnp.zeros_like(a)) for m in inside], axis=0)
            far = jnp.dot(one, basis, preferred_element_type=jnp.float32)
            for t in range(QUAD):
                row = place(clusters[first + t])
                table[row] += far[t * channels : (t + 1) * channels]
        return carry

    lax.fori_loop(0, senders, one_sender, 0, unroll=UNROLL)
    other[...] = table[other.shape[0] :]


def body(
    field,
    dest_group,
    src_local,
    ranks,
    mixing,
    v_factor,
    u_factor,
    slot_cluster,
    near_src,
    near_tgt,
    near_mixing,
    near_matrix,
):
    groups = lax.axis_size("tgt")
    shards = lax.axis_size("src")
    pairing = lax.axis_size("comp")
    blocks, rank_width, cluster = v_factor.shape
    comps, vectors, points = field.shape
    channels = comps * vectors
    owned = points // cluster
    slot_count = u_factor.shape[0]
    capacity = slot_count // groups
    near_count = near_matrix.shape[0]
    cores = 2
    chips = pairing * shards // cores
    kept = functools.partial(pltpu.with_memory_space_constraint, memory_space=pltpu.HBM)
    hbm = pl.BlockSpec(memory_space=pltpu.HBM)

    x = kept(field.reshape(channels, points))
    def place(w):
        c, j = lax.div(w, shards), lax.rem(w, shards)
        same = lax.rem(j, cores) == lax.rem(lax.axis_index("src"), cores)
        return lax.div(j, cores) * pairing + c + jnp.where(same, 0, chips)

    vmem = pl.BlockSpec(memory_space=pltpu.VMEM)
    table_shape = (cores * chips, channels, cluster)
    outgoing, u_near, near_table = pl.pallas_call(
        functools.partial(source_kernel, comps, place),
        out_shape=[
            jax.ShapeDtypeStruct((groups, channels, capacity * rank_width), jnp.bfloat16),
            jax.ShapeDtypeStruct(u_factor.shape, jnp.bfloat16),
            jax.ShapeDtypeStruct(table_shape, jnp.float32),
        ],
        in_specs=[hbm] * 11,
        out_specs=[vmem] * 3,
        scratch_shapes=[
            pltpu.SMEM((blocks,), jnp.int32),
            pltpu.SMEM((blocks,), jnp.int32),
            pltpu.SMEM((blocks,), jnp.int32),
            pltpu.SMEM((comps * comps, blocks), jnp.float32),
            pltpu.SMEM((near_count,), jnp.int32),
            pltpu.SMEM((near_count,), jnp.int32),
            pltpu.VMEM((comps, near_count, comps), jnp.float32),
            pltpu.VMEM((channels, points), jnp.bfloat16),
            pltpu.VMEM(near_matrix.shape, jnp.bfloat16),
            pltpu.VMEM(v_factor.shape, jnp.bfloat16),
            pltpu.VMEM((owned * channels, cluster), jnp.bfloat16),
            pltpu.SMEM((slot_count,), jnp.int32),
            pltpu.SMEM((slot_count // QUAD + TOGETHER,), jnp.int32),
            pltpu.SMEM((groups,), jnp.int32),
            pltpu.SemaphoreType.DMA((7 + comps * comps,)),
            pltpu.SemaphoreType.DMA((1 + 2 * PIECES,)),
        ],
        compiler_params=pltpu.CompilerParams(vmem_limit_bytes=SOURCE_MIB << 20),
        name="source",
    )(
        kept(dest_group[:, 0]),
        kept(src_local),
        kept(ranks),
        kept(mixing.transpose(1, 2, 0)),
        kept(near_src),
        kept(near_tgt),
        kept(near_mixing.transpose(1, 0, 2)),
        x,
        kept(near_matrix),
        kept(v_factor),
        kept(u_factor),
    )
    incoming = lax.all_to_all(outgoing, "tgt", split_axis=0, concat_axis=0, tiled=True)
    table, other = pl.pallas_call(
        functools.partial(target_kernel, place),
        out_shape=[
            jax.ShapeDtypeStruct(table_shape, jnp.float32),
            jax.ShapeDtypeStruct((chips, channels, cluster), jnp.float32),
        ],
        in_specs=[hbm] + [vmem] * 3,
        out_specs=[vmem] * 2,
        scratch_shapes=[pltpu.SMEM((slot_count,), jnp.int32), pltpu.SemaphoreType.DMA],
        input_output_aliases={3: 0},
        compiler_params=pltpu.CompilerParams(vmem_limit_bytes=TARGET_MIB << 20),
        name="target",
    )(kept(slot_cluster), u_near, incoming, near_table)
    mine = table[:chips]
    swapped = lax.ppermute(other, "src", [(j, j ^ 1) for j in range(shards)])
    sums = mine + swapped
    lines = [
        [c * shards + h * cores + k for h in range(shards // cores) for c in range(pairing)]
        for k in range(cores)
    ]
    row = lax.div(lax.axis_index("src"), cores) * pairing + lax.axis_index("comp")
    own = (jnp.arange(chips, dtype=jnp.int32) == row)[:, None, None]
    sending, own = lax.optimization_barrier((sums.astype(jnp.bfloat16), own))
    parts = lax.all_to_all(
        sending, ("comp", "src"), split_axis=0, concat_axis=0, tiled=True, axis_index_groups=lines
    )
    result = jnp.where(own, sums, parts.astype(jnp.float32)).sum(axis=0)
    return result.reshape(comps, vectors, cluster)


def solution(mesh):
    every = ("comp", "tgt", "src")
    placed = (
        P(None, None, ("tgt", "src")),
        P(every, None),
        P(every),
        P(every),
        P(every, None, None),
        P(every, None, None),
        P(every, None, None),
        P(every),
        P(every),
        P(every),
        P(every, None, None),
        P(every, None, None),
    )
    return jax.shard_map(
        body,
        mesh=mesh,
        in_specs=placed,
        out_specs=P(None, None, every),
        check_vma=False,
    )
```

```python
import functools

import jax
import jax.numpy as jnp
from jax import lax
from jax.experimental import pallas as pl
from jax.experimental.pallas import tpu as pltpu
from jax.sharding import PartitionSpec as P

SUB = 8
LANES = 128
QUAD = 4
TOGETHER = 8
PIECES = 4
UNROLL = 8
SOURCE_MIB = 20
TARGET_MIB = 20


def pieces(length):
    size = length // PIECES
    return [pl.ds(n * size, size) for n in range(PIECES)]


def spread(values, low):
    return jnp.concatenate(
        [jnp.where(low, values[t], values[t + 1]) for t in range(0, len(values), 2)], axis=-1
    )


def source_kernel(
    comps,
    place,
    dest_hbm,
    src_hbm,
    ranks_hbm,
    mixing_hbm,
    near_src_hbm,
    near_tgt_hbm,
    near_mixing_hbm,
    field_hbm,
    near_hbm,
    v_hbm,
    u_hbm,
    out,
    u,
    table,
    dest,
    src,
    ranks,
    mixing,
    near_src,
    near_tgt,
    near_mixing,
    field,
    near,
    v,
    x,
    slots,
    sets,
    counts,
    small_sems,
    big_sems,
):
    blocks, rank_width, cluster = v.shape
    groups, channels, lanes = out.shape
    rhs = channels // comps
    owned = x.shape[0] // channels
    capacity = slots.shape[0] // groups
    near_count = near.shape[0]

    pairs = [
        (dest_hbm, dest),
        (src_hbm, src),
        (ranks_hbm, ranks),
        (near_src_hbm, near_src),
        (near_tgt_hbm, near_tgt),
        (near_mixing_hbm, near_mixing),
        (field_hbm, field),
    ] + [
        (mixing_hbm.at[e, e2], mixing.at[e * comps + e2]) for e in range(comps) for e2 in range(comps)
    ]
    small = [pltpu.make_async_copy(p, q, small_sems.at[n]) for n, (p, q) in enumerate(pairs)]
    big = [
        pltpu.make_async_copy(p, q, big_sems.at[n])
        for n, (p, q) in enumerate(
            [(near_hbm, near)]
            + [(v_hbm.at[piece], v.at[piece]) for piece in pieces(blocks)]
            + [(u_hbm.at[piece], u.at[piece]) for piece in pieces(slots.shape[0])]
        )
    ]
    for copy in small + big[: 1 + PIECES]:
        copy.start()
    table[...] = jnp.zeros_like(table)
    out[...] = jnp.zeros_like(out)
    for g in range(groups):
        counts[g] = 0
    for copy in small:
        copy.wait()

    def put(b, carry):
        g = dest[b]
        k = counts[g]
        counts[g] = k + 1
        slots[g * capacity + k] = b
        return carry

    lax.fori_loop(0, blocks, put, 0, unroll=8)
    used = jnp.int32(0)
    for g in range(groups):
        for q in range(capacity // QUAD):
            sets[used] = g * (capacity // QUAD) + q
            used = used + (counts[g] > q * QUAD).astype(jnp.int32)
    for n in range(TOGETHER):
        sets[used + n] = sets[0]
    for s in range(owned):
        x[s * channels : (s + 1) * channels, :] = field[:, s * cluster : (s + 1) * cluster]
    big[0].wait()
    for n in range(near_count):
        begin = pl.multiple_of(near_src[n] * channels, channels)
        y = lax.dot_general(
            x[pl.ds(begin, channels), :],
            near[n],
            (((1,), (1,)), ((), ())),
            preferred_element_type=jnp.float32,
        )
        parts = [y[e * rhs : (e + 1) * rhs] for e in range(comps)]
        row = place(near_tgt[n])
        for e in range(comps):
            total = None
            for e2 in range(comps):
                term = near_mixing[e, n : n + 1, e2 : e2 + 1] * parts[e2]
                total = term if total is None else total + term
            table[row, e * rhs : (e + 1) * rhs, :] += total
    for copy in big[1 : 1 + PIECES]:
        copy.wait()
    for copy in big[1 + PIECES :]:
        copy.start()

    width = QUAD * rank_width
    low = lax.broadcasted_iota(jnp.int32, (SUB, LANES), 1) < rank_width
    within = lax.broadcasted_iota(jnp.int32, (SUB, width), 1) & (rank_width - 1)

    def one_set(number):
        g = lax.div(number, capacity // QUAD)
        begin = lax.rem(number, capacity // QUAD) * QUAD
        count = counts[g]
        first = number * QUAD
        full = [count > begin + t for t in range(QUAD)]
        ids = [jnp.where(full[t], slots[first + t], 0) for t in range(QUAD)]
        basis = jnp.concatenate([v[b] for b in ids], axis=0)
        y = lax.dot_general(
            x[...], basis, (((1,), (1,)), ((), ())), preferred_element_type=jnp.float32
        ).reshape(owned, comps, rhs // SUB, SUB, width)
        which = spread([src[b] for b in ids], low)
        picked = y[0]
        for s in range(1, owned):
            picked = jnp.where(which == s, y[s], picked)
        limit = spread([jnp.where(full[t], ranks[ids[t]], 0) for t in range(QUAD)], low)
        kept = within < limit
        cols = pl.ds(pl.multiple_of(begin * rank_width, width), width)
        for e in range(comps):
            total = None
            for e2 in range(comps):
                m = spread([mixing[e * comps + e2, b] for b in ids], low)
                m = jnp.where(kept, m, 0.0)
                term = m * picked[e2]
                total = term if total is None else total + term
            out[g, e * rhs : (e + 1) * rhs, cols] = total.reshape(rhs, width).astype(out.dtype)

    def one_pass(n, carry):
        for m in range(TOGETHER):
            one_set(sets[n * TOGETHER + m])
        return carry

    lax.fori_loop(0, lax.div(used + TOGETHER - 1, TOGETHER), one_pass, 0)
    for copy in big[1 + PIECES :]:
        copy.wait()


def target_kernel(place, clusters_hbm, u, sent, near_table, table, other, clusters, sem):
    senders, channels, lanes = sent.shape
    slot_count, rank_width, cluster = u.shape
    capacity = slot_count // senders
    width = QUAD * rank_width
    copy = pltpu.make_async_copy(clusters_hbm, clusters, sem)
    copy.start()
    lane = lax.broadcasted_iota(jnp.int32, (1, width), 1)
    inside = [(lane >= t * rank_width) & (lane < (t + 1) * rank_width) for t in range(QUAD)]
    copy.wait()

    def one_sender(i, carry):
        for q in range(capacity // QUAD):
            a = sent[i, :, q * width : (q + 1) * width]
            first = i * capacity + q * QUAD
            basis = u[pl.ds(first, QUAD)].reshape(width, cluster)
            one = jnp.concatenate([jnp.where(m, a, jnp.zeros_like(a)) for m in inside], axis=0)
            far = jnp.dot(one, basis, preferred_element_type=jnp.float32)
            for t in range(QUAD):
                row = place(clusters[first + t])
                table[row] += far[t * channels : (t + 1) * channels]
        return carry

    lax.fori_loop(0, senders, one_sender, 0, unroll=UNROLL)
    other[...] = table[other.shape[0] :]


def body(
    field,
    dest_group,
    src_local,
    ranks,
    mixing,
    v_factor,
    u_factor,
    slot_cluster,
    near_src,
    near_tgt,
    near_mixing,
    near_matrix,
):
    groups = lax.axis_size("tgt")
    shards = lax.axis_size("src")
    pairing = lax.axis_size("comp")
    blocks, rank_width, cluster = v_factor.shape
    comps, vectors, points = field.shape
    channels = comps * vectors
    owned = points // cluster
    slot_count = u_factor.shape[0]
    capacity = slot_count // groups
    near_count = near_matrix.shape[0]
    cores = 2
    chips = pairing * shards // cores
    kept = functools.partial(pltpu.with_memory_space_constraint, memory_space=pltpu.HBM)
    hbm = pl.BlockSpec(memory_space=pltpu.HBM)

    x = kept(field.reshape(channels, points))
    def place(w):
        c, j = lax.div(w, shards), lax.rem(w, shards)
        same = lax.rem(j, cores) == lax.rem(lax.axis_index("src"), cores)
        return lax.div(j, cores) * pairing + c + jnp.where(same, 0, chips)

    vmem = pl.BlockSpec(memory_space=pltpu.VMEM)
    table_shape = (cores * chips, channels, cluster)
    outgoing, u_near, near_table = pl.pallas_call(
        functools.partial(source_kernel, comps, place),
        out_shape=[
            jax.ShapeDtypeStruct((groups, channels, capacity * rank_width), jnp.bfloat16),
            jax.ShapeDtypeStruct(u_factor.shape, jnp.bfloat16),
            jax.ShapeDtypeStruct(table_shape, jnp.float32),
        ],
        in_specs=[hbm] * 11,
        out_specs=[vmem] * 3,
        scratch_shapes=[
            pltpu.SMEM((blocks,), jnp.int32),
            pltpu.SMEM((blocks,), jnp.int32),
            pltpu.SMEM((blocks,), jnp.int32),
            pltpu.SMEM((comps * comps, blocks), jnp.float32),
            pltpu.SMEM((near_count,), jnp.int32),
            pltpu.SMEM((near_count,), jnp.int32),
            pltpu.VMEM((comps, near_count, comps), jnp.float32),
            pltpu.VMEM((channels, points), jnp.bfloat16),
            pltpu.VMEM(near_matrix.shape, jnp.bfloat16),
            pltpu.VMEM(v_factor.shape, jnp.bfloat16),
            pltpu.VMEM((owned * channels, cluster), jnp.bfloat16),
            pltpu.SMEM((slot_count,), jnp.int32),
            pltpu.SMEM((slot_count // QUAD + TOGETHER,), jnp.int32),
            pltpu.SMEM((groups,), jnp.int32),
            pltpu.SemaphoreType.DMA((7 + comps * comps,)),
            pltpu.SemaphoreType.DMA((1 + 2 * PIECES,)),
        ],
        compiler_params=pltpu.CompilerParams(vmem_limit_bytes=SOURCE_MIB << 20),
        name="source",
    )(
        kept(dest_group[:, 0]),
        kept(src_local),
        kept(ranks),
        kept(mixing.transpose(1, 2, 0)),
        kept(near_src),
        kept(near_tgt),
        kept(near_mixing.transpose(1, 0, 2)),
        x,
        kept(near_matrix),
        kept(v_factor),
        kept(u_factor),
    )
    incoming = lax.all_to_all(outgoing, "tgt", split_axis=0, concat_axis=0, tiled=True)
    table, other = pl.pallas_call(
        functools.partial(target_kernel, place),
        out_shape=[
            jax.ShapeDtypeStruct(table_shape, jnp.float32),
            jax.ShapeDtypeStruct((chips, channels, cluster), jnp.float32),
        ],
        in_specs=[hbm] + [vmem] * 3,
        out_specs=[vmem] * 2,
        scratch_shapes=[pltpu.SMEM((slot_count,), jnp.int32), pltpu.SemaphoreType.DMA],
        input_output_aliases={3: 0},
        compiler_params=pltpu.CompilerParams(vmem_limit_bytes=TARGET_MIB << 20),
        name="target",
    )(kept(slot_cluster), u_near, incoming, near_table)
    mine = table[:chips]
    swapped = lax.ppermute(other, "src", [(j, j ^ 1) for j in range(shards)])
    sums = mine + swapped
    lines = [
        [c * shards + h * cores + k for h in range(shards // cores) for c in range(pairing)]
        for k in range(cores)
    ]
    row = lax.div(lax.axis_index("src"), cores) * pairing + lax.axis_index("comp")
    own = (jnp.arange(chips, dtype=jnp.int32) == row)[:, None, None]
    sending, own = lax.optimization_barrier((sums.astype(jnp.bfloat16), own))
    parts = lax.all_to_all(
        sending, ("comp", "src"), split_axis=0, concat_axis=0, tiled=True, axis_index_groups=lines
    )
    result = jnp.where(own, sums, parts.astype(jnp.float32)).sum(axis=0)
    return result.reshape(comps, vectors, cluster)


def solution(mesh):
    every = ("comp", "tgt", "src")
    placed = (
        P(None, None, ("tgt", "src")),
        P(every, None),
        P(every),
        P(every),
        P(every, None, None),
        P(every, None, None),
        P(every, None, None),
        P(every),
        P(every),
        P(every),
        P(every, None, None),
        P(every, None, None),
    )
    return jax.shard_map(
        body,
        mesh=mesh,
        in_specs=placed,
        out_specs=P(None, None, every),
        check_vma=False,
    )
```

```python
import functools

import jax
import jax.numpy as jnp
from jax import lax
from jax.experimental import pallas as pl
from jax.experimental.pallas import tpu as pltpu
from jax.sharding import PartitionSpec as P

SUB = 8
LANES = 128
QUAD = 4
TOGETHER = 8
PIECES = 4
UNROLL = 8
SOURCE_MIB = 20
TARGET_MIB = 20


def pieces(length):
    size = length // PIECES
    return [pl.ds(n * size, size) for n in range(PIECES)]


def spread(values, low):
    return jnp.concatenate(
        [jnp.where(low, values[t], values[t + 1]) for t in range(0, len(values), 2)], axis=-1
    )


def source_kernel(
    comps,
    place,
    dest_hbm,
    src_hbm,
    ranks_hbm,
    mixing_hbm,
    near_src_hbm,
    near_tgt_hbm,
    near_mixing_hbm,
    field_hbm,
    near_hbm,
    v_hbm,
    u_hbm,
    out,
    u,
    table,
    dest,
    src,
    ranks,
    mixing,
    near_src,
    near_tgt,
    near_mixing,
    field,
    near,
    v,
    x,
    slots,
    sets,
    counts,
    small_sems,
    big_sems,
):
    blocks, rank_width, cluster = v.shape
    groups, channels, lanes = out.shape
    rhs = channels // comps
    owned = x.shape[0] // channels
    capacity = slots.shape[0] // groups
    near_count = near.shape[0]

    pairs = [
        (dest_hbm, dest),
        (src_hbm, src),
        (ranks_hbm, ranks),
        (near_src_hbm, near_src),
        (near_tgt_hbm, near_tgt),
        (near_mixing_hbm, near_mixing),
        (field_hbm, field),
    ] + [
        (mixing_hbm.at[e, e2], mixing.at[e * comps + e2]) for e in range(comps) for e2 in range(comps)
    ]
    small = [pltpu.make_async_copy(p, q, small_sems.at[n]) for n, (p, q) in enumerate(pairs)]
    big = [
        pltpu.make_async_copy(p, q, big_sems.at[n])
        for n, (p, q) in enumerate(
            [(near_hbm, near)]
            + [(v_hbm.at[piece], v.at[piece]) for piece in pieces(blocks)]
            + [(u_hbm.at[piece], u.at[piece]) for piece in pieces(slots.shape[0])]
        )
    ]
    for copy in small + big[: 1 + PIECES]:
        copy.start()
    table[...] = jnp.zeros_like(table)
    out[...] = jnp.zeros_like(out)
    for g in range(groups):
        counts[g] = 0
    for copy in small:
        copy.wait()

    def put(b, carry):
        g = dest[b]
        k = counts[g]
        counts[g] = k + 1
        slots[g * capacity + k] = b
        return carry

    lax.fori_loop(0, blocks, put, 0, unroll=8)
    used = jnp.int32(0)
    for g in range(groups):
        for q in range(capacity // QUAD):
            sets[used] = g * (capacity // QUAD) + q
            used = used + (counts[g] > q * QUAD).astype(jnp.int32)
    for n in range(TOGETHER):
        sets[used + n] = sets[0]
    for s in range(owned):
        x[s * channels : (s + 1) * channels, :] = field[:, s * cluster : (s + 1) * cluster]
    big[0].wait()
    for n in range(near_count):
        begin = pl.multiple_of(near_src[n] * channels, channels)
        y = lax.dot_general(
            x[pl.ds(begin, channels), :],
            near[n],
            (((1,), (1,)), ((), ())),
            preferred_element_type=jnp.float32,
        )
        parts = [y[e * rhs : (e + 1) * rhs] for e in range(comps)]
        row = place(near_tgt[n])
        for e in range(comps):
            total = None
            for e2 in range(comps):
                term = near_mixing[e, n : n + 1, e2 : e2 + 1] * parts[e2]
                total = term if total is None else total + term
            table[row, e * rhs : (e + 1) * rhs, :] += total
    for copy in big[1 : 1 + PIECES]:
        copy.wait()
    for copy in big[1 + PIECES :]:
        copy.start()

    width = QUAD * rank_width
    low = lax.broadcasted_iota(jnp.int32, (SUB, LANES), 1) < rank_width
    within = lax.broadcasted_iota(jnp.int32, (SUB, width), 1) & (rank_width - 1)

    def one_set(number):
        g = lax.div(number, capacity // QUAD)
        begin = lax.rem(number, capacity // QUAD) * QUAD
        count = counts[g]
        first = number * QUAD
        full = [count > begin + t for t in range(QUAD)]
        ids = [jnp.where(full[t], slots[first + t], 0) for t in range(QUAD)]
        basis = jnp.concatenate([v[b] for b in ids], axis=0)
        y = lax.dot_general(
            x[...], basis, (((1,), (1,)), ((), ())), preferred_element_type=jnp.float32
        ).reshape(owned, comps, rhs // SUB, SUB, width)
        which = spread([src[b] for b in ids], low)
        picked = y[0]
        for s in range(1, owned):
            picked = jnp.where(which == s, y[s], picked)
        limit = spread([jnp.where(full[t], ranks[ids[t]], 0) for t in range(QUAD)], low)
        kept = within < limit
        cols = pl.ds(pl.multiple_of(begin * rank_width, width), width)
        for e in range(comps):
            total = None
            for e2 in range(comps):
                m = spread([mixing[e * comps + e2, b] for b in ids], low)
                m = jnp.where(kept, m, 0.0)
                term = m * picked[e2]
                total = term if total is None else total + term
            out[g, e * rhs : (e + 1) * rhs, cols] = total.reshape(rhs, width).astype(out.dtype)

    def one_pass(n, carry):
        for m in range(TOGETHER):
            one_set(sets[n * TOGETHER + m])
        return carry

    lax.fori_loop(0, lax.div(used + TOGETHER - 1, TOGETHER), one_pass, 0)
    for copy in big[1 + PIECES :]:
        copy.wait()


def target_kernel(place, clusters_hbm, u, sent, near_table, table, other, clusters, sem):
    senders, channels, lanes = sent.shape
    slot_count, rank_width, cluster = u.shape
    capacity = slot_count // senders
    width = QUAD * rank_width
    copy = pltpu.make_async_copy(clusters_hbm, clusters, sem)
    copy.start()
    lane = lax.broadcasted_iota(jnp.int32, (1, width), 1)
    inside = [(lane >= t * rank_width) & (lane < (t + 1) * rank_width) for t in range(QUAD)]
    copy.wait()

    def one_sender(i, carry):
        for q in range(capacity // QUAD):
            a = sent[i, :, q * width : (q + 1) * width]
            first = i * capacity + q * QUAD
            basis = u[pl.ds(first, QUAD)].reshape(width, cluster)
            one = jnp.concatenate([jnp.where(m, a, jnp.zeros_like(a)) for m in inside], axis=0)
            far = jnp.dot(one, basis, preferred_element_type=jnp.float32)
            for t in range(QUAD):
                row = place(clusters[first + t])
                table[row] += far[t * channels : (t + 1) * channels]
        return carry

    lax.fori_loop(0, senders, one_sender, 0, unroll=UNROLL)
    other[...] = table[other.shape[0] :]


def combine_kernel(table, swapped, own, *sending):
    own[...] = table[0] + swapped[0]
    for n, part in enumerate(sending, 1):
        part[...] = (table[n] + swapped[n]).astype(part.dtype)


def body(
    field,
    dest_group,
    src_local,
    ranks,
    mixing,
    v_factor,
    u_factor,
    slot_cluster,
    near_src,
    near_tgt,
    near_mixing,
    near_matrix,
):
    groups = lax.axis_size("tgt")
    shards = lax.axis_size("src")
    pairing = lax.axis_size("comp")
    blocks, rank_width, cluster = v_factor.shape
    comps, vectors, points = field.shape
    channels = comps * vectors
    owned = points // cluster
    slot_count = u_factor.shape[0]
    capacity = slot_count // groups
    near_count = near_matrix.shape[0]
    cores = 2
    chips = pairing * shards // cores
    kept = functools.partial(pltpu.with_memory_space_constraint, memory_space=pltpu.HBM)
    hbm = pl.BlockSpec(memory_space=pltpu.HBM)

    x = kept(field.reshape(channels, points))
    def place(w):
        c, j = lax.div(w, shards), lax.rem(w, shards)
        mine = lax.axis_index("src")
        same = lax.rem(j, cores) == lax.rem(mine, cores)
        here = lax.div(mine, cores) * pairing + lax.axis_index("comp")
        up = lax.div(j, cores) * pairing + c - here + chips
        return lax.rem(up, chips) + jnp.where(same, 0, chips)

    vmem = pl.BlockSpec(memory_space=pltpu.VMEM)
    table_shape = (cores * chips, channels, cluster)
    outgoing, u_near, near_table = pl.pallas_call(
        functools.partial(source_kernel, comps, place),
        out_shape=[
            jax.ShapeDtypeStruct((groups, channels, capacity * rank_width), jnp.bfloat16),
            jax.ShapeDtypeStruct(u_factor.shape, jnp.bfloat16),
            jax.ShapeDtypeStruct(table_shape, jnp.float32),
        ],
        in_specs=[hbm] * 11,
        out_specs=[vmem] * 3,
        scratch_shapes=[
            pltpu.SMEM((blocks,), jnp.int32),
            pltpu.SMEM((blocks,), jnp.int32),
            pltpu.SMEM((blocks,), jnp.int32),
            pltpu.SMEM((comps * comps, blocks), jnp.float32),
            pltpu.SMEM((near_count,), jnp.int32),
            pltpu.SMEM((near_count,), jnp.int32),
            pltpu.VMEM((comps, near_count, comps), jnp.float32),
            pltpu.VMEM((channels, points), jnp.bfloat16),
            pltpu.VMEM(near_matrix.shape, jnp.bfloat16),
            pltpu.VMEM(v_factor.shape, jnp.bfloat16),
            pltpu.VMEM((owned * channels, cluster), jnp.bfloat16),
            pltpu.SMEM((slot_count,), jnp.int32),
            pltpu.SMEM((slot_count // QUAD + TOGETHER,), jnp.int32),
            pltpu.SMEM((groups,), jnp.int32),
            pltpu.SemaphoreType.DMA((7 + comps * comps,)),
            pltpu.SemaphoreType.DMA((1 + 2 * PIECES,)),
        ],
        compiler_params=pltpu.CompilerParams(vmem_limit_bytes=SOURCE_MIB << 20),
        name="source",
    )(
        kept(dest_group[:, 0]),
        kept(src_local),
        kept(ranks),
        kept(mixing.transpose(1, 2, 0)),
        kept(near_src),
        kept(near_tgt),
        kept(near_mixing.transpose(1, 0, 2)),
        x,
        kept(near_matrix),
        kept(v_factor),
        kept(u_factor),
    )
    incoming = lax.all_to_all(outgoing, "tgt", split_axis=0, concat_axis=0, tiled=True)
    table, other = pl.pallas_call(
        functools.partial(target_kernel, place),
        out_shape=[
            jax.ShapeDtypeStruct(table_shape, jnp.float32),
            jax.ShapeDtypeStruct((chips, channels, cluster), jnp.float32),
        ],
        in_specs=[hbm] + [vmem] * 3,
        out_specs=[vmem] * 2,
        scratch_shapes=[pltpu.SMEM((slot_count,), jnp.int32), pltpu.SemaphoreType.DMA],
        input_output_aliases={3: 0},
        compiler_params=pltpu.CompilerParams(vmem_limit_bytes=TARGET_MIB << 20),
        name="target",
    )(kept(slot_cluster), u_near, incoming, near_table)
    swapped = lax.ppermute(other, "src", [(j, j ^ 1) for j in range(shards)])
    own, *sending = pl.pallas_call(
        combine_kernel,
        out_shape=[jax.ShapeDtypeStruct((channels, cluster), jnp.float32)]
        + [jax.ShapeDtypeStruct((channels, cluster), jnp.bfloat16)] * (chips - 1),
        in_specs=[vmem] * 2,
        out_specs=[vmem] * chips,
        compiler_params=pltpu.CompilerParams(vmem_limit_bytes=8 << 20),
        name="combine",
    )(table, swapped)

    def device(z, core):
        return (z % pairing) * shards + (z // pairing) * cores + core

    result = own
    for up in sorted(range(1, chips), key=lambda n: -min(n, chips - n)):
        part = sending[up - 1]
        moves = [
            (device(z, core), device((z + up) % chips, core))
            for z in range(chips)
            for core in range(cores)
        ]
        result = result + lax.ppermute(part, ("comp", "src"), moves).astype(jnp.float32)
    return result.reshape(comps, vectors, cluster)


def solution(mesh):
    every = ("comp", "tgt", "src")
    placed = (
        P(None, None, ("tgt", "src")),
        P(every, None),
        P(every),
        P(every),
        P(every, None, None),
        P(every, None, None),
        P(every, None, None),
        P(every),
        P(every),
        P(every),
        P(every, None, None),
        P(every, None, None),
    )
    return jax.shard_map(
        body,
        mesh=mesh,
        in_specs=placed,
        out_specs=P(None, None, every),
        check_vma=False,
    )
```
